32 devices in a mesh: groups: 1, ep: 32 (over z, y, x, core).
Axes of the slice: x: 2, y: 2, z: 4, core: 2. Of those that a mesh axis runs over, the one named last changes fastest.
Arguments:
- queries: bfloat16 [128, 8, 16, 576], P(('groups', 'ep')), may hold values from -48 to 48
- cache: bfloat16 [128, 384, 576], P(('groups', 'ep')), may hold values from -4 to 4
- drafts: bfloat16 [128, 8, 576], P(('groups', 'ep')), may hold values from -8 to 8
- lengths: int32 [128], P(('groups', 'ep')), may hold values from 96 to 384
- value_up: bfloat16 [16, 512, 128], replicated, may hold values from -0.25 to 0.25
- residual: bfloat16 [1024, 2048], P(('groups', 'ep')), may hold values from -20 to 20
- norm_gain: float32 [2048], replicated, may hold values from 0.5 to 1.5
- w_gate: bfloat16 [32, 2048, 704], P('ep'), may hold values from -0.125 to 0.125
- w_up: bfloat16 [32, 2048, 704], P('ep'), may hold values from -0.125 to 0.125
- w_down: bfloat16 [32, 704, 2048], P('ep'), may hold values from -0.15625 to 0.15625
- routes: int32 [1024, 6], P(('groups', 'ep')), may hold values from 0 to 15, all different within a row; in each aligned block of 32 rows (0 to 31, 32 to 63, ...) at most 14 rows name the same one
- combine_weights: float32 [1024, 6], P(('groups', 'ep')), may hold values from 0.05 to 0.4
Outputs:
- layer_out: bfloat16 [1024, 2048], P(('groups', 'ep'))
The draws below stay inside these ranges and needn't reach their ends.
Inputs may be any that keep to these rules, and one draw needn't show every extreme that they name: `routes`: among the rows of one device, no expert is named more than 14 times over all slots.
All inputs are finite; a program needn't handle non-finite values.
Results may differ from the reference program's by a relative error of at most 0.0043.
Values may be sent and summed in bfloat16 or wider, within the bound.
A program may use at most 64 MiB of HBM per device.

```python
import math
import jax
import jax.numpy as jnp
import numpy as np
from jax import lax

D = 2048
H = 16
LAT = 512
ROPE = 64
VDIM = 128
FF = 1408
TOP = 6
DRAFT = 8
CACHE = 384
EXPERTS = 16
FF_HALF = 704
TOK_DEV = 32
REQS = 128
TOKENS = 1024
CAP = 14
N_EP = 32


def base_cache(key):
    first = jax.random.fold_in(key, 11)
    shape = (REQS, CACHE, LAT + ROPE)
    values = jnp.clip(jax.random.normal(first, shape, jnp.float32), -4.0, 4.0)
    return values


def draw_cache(key, part):
    values = base_cache(key)
    return jnp.clip(values, -4.0, 4.0).astype(jnp.bfloat16)


def draw_queries(key, part):
    shape = (REQS, DRAFT, H, LAT + ROPE)
    values = jnp.clip(jax.random.normal(jax.random.fold_in(key, 14), shape, jnp.float32), -4.0, 4.0)
    return values.astype(jnp.bfloat16)


def draw_residual(key, part):
    shape = (TOKENS, D)
    rows = jnp.exp(jax.random.uniform(jax.random.fold_in(key, 21), (TOKENS, 1), jnp.float32, -1.386, 0.916))
    columns = jnp.exp(jax.random.uniform(jax.random.fold_in(key, 22), (1, D), jnp.float32, -0.693, 0.693))
    base = jnp.clip(jax.random.normal(jax.random.fold_in(key, 24), shape, jnp.float32), -4.0, 4.0)
    return jnp.clip(base * rows * columns, -20.0, 20.0).astype(jnp.bfloat16)


def with_ends(drawn, own_key, low, largest):
    dims = drawn.shape
    spot = [jax.random.randint(jax.random.fold_in(own_key, axis), (), 0, dims[axis]) for axis in range(len(dims))]
    drawn = drawn.at[tuple(spot)].set(low)
    longest = dims.index(max(dims))
    spot[longest] = (spot[longest] + 1) % dims[longest]
    return drawn.at[tuple(spot)].set(largest)


def block_levels(stream_key, shape, split, least, top_value):
    loudness, own = 1.0, jax.random.fold_in(stream_key, 6)
    for position, parts in split:
        draws = jnp.exp(jax.random.uniform(jax.random.fold_in(own, position), (parts,), jnp.float32, least / len(split), top_value / len(split)))
        loudness = loudness * jnp.repeat(draws, shape[position] // parts).reshape([-1 if axis == position else 1 for axis in range(len(shape))])
    return loudness


def routed_block(stream_key, own, number, rows, count, top, bound, slope):
    ranking = jax.random.permutation(stream_key, count)
    heavy_load, usual = portions_of(count, rows * top, bound, slope, True), portions_of(count, rows * top, bound, slope, False)
    places = jnp.arange(count)

    def named(tallies, turn):
        used = int((tallies > 0).sum())
        fixed = max(1, used // 4)
        shifted = fixed + (places - fixed + turn * (used - fixed)) % max(1, count - fixed)
        return jnp.zeros((count,), jnp.int32).at[ranking[jnp.where(places < fixed, places, shifted)]].set(jnp.asarray(tallies, jnp.int32))

    tallies = jnp.where(number % 4 == 0, named(heavy_load, number // 4), named(usual, number - number // 4 - 1))
    mixed = jax.random.permutation(jax.random.fold_in(own, 3), count)
    donor, taker = mixed[0:count // 2 * 2:2], mixed[1:count // 2 * 2:2]
    slack = jnp.minimum(tallies[donor] - 1, bound - tallies[taker]) // 2
    slack = jnp.where((donor == ranking[0]) | (taker == ranking[0]) | (tallies[taker] == 0), 0, jnp.maximum(slack, 0))
    shifted = jax.random.randint(jax.random.fold_in(own, 4), (count // 2,), 0, 1 << 20) % (slack + 1)
    tallies = tallies.at[donor].add(-shifted).at[taker].add(shifted)
    labels = jnp.searchsorted(jnp.cumsum(tallies), jnp.arange(rows * top), side="right").astype(jnp.int32)
    table = labels.reshape(top, rows).T
    table = table[jax.random.permutation(jax.random.fold_in(own, 1), rows)]
    turn = jax.random.randint(jax.random.fold_in(own, 2), (rows, 1), 0, top)
    return jnp.take_along_axis(table, (jnp.arange(top)[None, :] + turn) % top, axis=1)


def portions_of(number_of, total, most, lean, full):
    loads = [(1 << 20) // math.isqrt(grade ** lean) + 1 for grade in range(1, number_of + 1)]
    largest = most if full else min(most, max(-(-total // number_of), total * loads[0] // sum(loads)))
    least = 1 if total - largest >= number_of - 1 else 0
    holding, rest = [largest] + [least] * (number_of - 1), total - largest - least * (number_of - 1)
    while rest > 0:
        movable = [i for i in range(1, number_of) if holding[i] < largest] or [i for i in range(1, number_of) if holding[i] < most]
        mass, budget = sum([loads[i] for i in movable]), rest
        for i in movable:
            more = min(most - holding[i], max(1, budget * loads[i] // mass), rest)
            holding[i] = holding[i] + more
            rest = rest - more
    return np.array(holding)


def bell_draw(own_key, extent, scale, reach, cuts=(), kind=jnp.bfloat16):
    drawn = scale * jax.random.normal(own_key, extent, jnp.float32)
    if cuts:
        drawn = drawn * block_levels(own_key, extent, cuts, -0.22, 0.18)
    return jnp.clip(drawn, -reach, reach).astype(kind)


def setup_inputs(seed: int = 0, part: int = 0) -> dict:
    streams_of = jax.random.split(jax.random.key(seed), 13)
    part_splits = jax.random.split(jax.random.fold_in(streams_of[12], part), 13)
    queries = draw_queries(jax.random.fold_in(jax.random.fold_in(streams_of[12], part), 71), part)
    cache = draw_cache(jax.random.fold_in(jax.random.fold_in(streams_of[12], part), 71), part)
    drafts = bell_draw(part_splits[2], (REQS, DRAFT, LAT + ROPE), 2.0, 8.0, ((0, 32),))
    lengths = with_ends(jax.random.randint(part_splits[3], (REQS,), CACHE // 4, CACHE + 1), jax.random.fold_in(part_splits[3], 1), CACHE // 4, CACHE).astype(jnp.int32)
    value_up = bell_draw(streams_of[4], (H, LAT, VDIM), LAT ** -0.5, 0.25)
    residual = draw_residual(jax.random.fold_in(jax.random.fold_in(streams_of[12], part), 71), part)
    norm_gain = jnp.clip(1.0 + 0.1 * jax.random.normal(streams_of[6], (D,), jnp.float32), 0.5, 1.5)
    w_gate = bell_draw(streams_of[7], (2 * EXPERTS, D, FF_HALF), D ** -0.5, 0.125, ((0, 32),))
    w_up = bell_draw(streams_of[8], (2 * EXPERTS, D, FF_HALF), D ** -0.5, 0.125, ((0, 32),))
    w_down = bell_draw(streams_of[9], (2 * EXPERTS, FF_HALF, D), FF ** -0.5, 0.15625, ((0, 32),))
    routes_keys = jax.random.split(jax.random.fold_in(part_splits[10], 1), TOKENS // TOK_DEV)
    routes_turns = jax.random.permutation(jax.random.fold_in(part_splits[10], 3), TOKENS // TOK_DEV)
    routes = jax.vmap(lambda own, number: routed_block(jax.random.fold_in(part_splits[10], 2), own, number, TOK_DEV, EXPERTS, TOP, CAP, 2))(routes_keys, routes_turns).reshape((TOKENS, TOP))
    combine_weights = jnp.clip(0.05 + 0.35 * jax.random.uniform(part_splits[11], (TOKENS, TOP), jnp.float32) ** block_levels(part_splits[11], (TOKENS, TOP), ((0, 32),), -0.2, 0.2), 0.05, 0.4)
    return {"queries": queries, "cache": cache, "drafts": drafts, "lengths": lengths, "value_up": value_up, "residual": residual, "norm_gain": norm_gain, "w_gate": w_gate, "w_up": w_up, "w_down": w_down, "routes": routes, "combine_weights": combine_weights}


def attend(queries, cache, drafts, lengths, value_up):
    reqs, draft, heads, width = queries.shape
    latent = value_up.shape[1]
    scale = (VDIM + ROPE) ** (-0.5)
    q_full = queries.astype(jnp.float32)
    c_full = cache.astype(jnp.float32)
    d_full = drafts.astype(jnp.float32)
    cached = jnp.einsum('rjhk,rck->rjhc', q_full, c_full) * scale
    own = jnp.einsum('rjhk,rik->rjhi', q_full, d_full) * scale
    visible = (jnp.arange(cache.shape[1], dtype=jnp.int32)[None, :] < lengths[:, None])[:, None, None, :]
    causal = (jnp.arange(draft, dtype=jnp.int32)[None, :] <= jnp.arange(draft, dtype=jnp.int32)[:, None])[None, :, None, :]
    cached = jnp.where(visible, cached, -1e+30)
    own = jnp.where(causal, own, -1e+30)
    highest = jnp.maximum(lax.optimization_barrier(jnp.max(cached, axis=-1, keepdims=True)), lax.optimization_barrier(jnp.max(own, axis=-1, keepdims=True)))
    e_cached = jnp.where(visible, jnp.exp(cached - highest), 0.0)
    e_own = jnp.where(causal, jnp.exp(own - highest), 0.0)
    total = lax.optimization_barrier(jnp.sum(e_cached, axis=-1, keepdims=True)) + lax.optimization_barrier(jnp.sum(e_own, axis=-1, keepdims=True))
    p_cached = (e_cached / total).astype(jnp.bfloat16).astype(jnp.float32)
    p_own = (e_own / total).astype(jnp.bfloat16).astype(jnp.float32)
    mixed = jnp.einsum('rjhc,rcl->rjhl', p_cached, c_full[..., :latent]) + jnp.einsum('rjhi,ril->rjhl', p_own, d_full[..., :latent])
    mixed = mixed.astype(jnp.bfloat16).astype(jnp.float32)
    heads_out = jnp.einsum('rjhl,hlv->rjhv', mixed, value_up.astype(jnp.float32))
    return heads_out.reshape(reqs * draft, heads * value_up.shape[2])

def run_expert(items):
    rows, gate_w, up_w, down_w = items
    total = jnp.zeros((rows.shape[0], down_w.shape[2]), jnp.float32)
    for half in range(2):
        gate = jnp.dot(rows, gate_w[half], preferred_element_type=jnp.float32)
        upper = jnp.dot(rows, up_w[half], preferred_element_type=jnp.float32)
        active = (jax.nn.silu(gate) * upper).astype(jnp.bfloat16)
        total = total + jnp.dot(active, down_w[half], preferred_element_type=jnp.float32)
    return total.astype(jnp.bfloat16)

def reference(queries, cache, drafts, lengths, value_up, residual, norm_gain, w_gate, w_up, w_down, routes, combine_weights):
    attended = attend(queries, cache, drafts, lengths, value_up)
    stream = residual.astype(jnp.float32) + attended
    normed = (stream * lax.rsqrt(lax.optimization_barrier(jnp.mean(stream * stream, axis=-1, keepdims=True)) + 1e-06) * norm_gain).astype(jnp.bfloat16)
    flat = routes.reshape(N_EP, TOK_DEV * TOP)
    onehot = (flat[:, :, None] == jnp.arange(EXPERTS, dtype=jnp.int32)[None, None, :]).astype(jnp.int32)
    rank = jnp.cumsum(onehot, axis=1) - onehot
    slot = lax.optimization_barrier(jnp.sum(rank * onehot, axis=-1)).astype(jnp.int32)
    rowpos = (jnp.arange(N_EP, dtype=jnp.int32)[:, None] * CAP + slot).astype(jnp.int32)
    token = (jnp.arange(N_EP, dtype=jnp.int32)[:, None] * TOK_DEV + jnp.arange(TOK_DEV * TOP, dtype=jnp.int32)[None, :] // TOP).astype(jnp.int32)
    buffer = jnp.zeros((EXPERTS, N_EP * CAP, D), jnp.bfloat16)
    buffer = buffer.at[flat.reshape(-1), rowpos.reshape(-1)].set(normed[token.reshape(-1)])
    gate_w = w_gate.reshape(EXPERTS, 2, D, FF_HALF)
    up_w = w_up.reshape(EXPERTS, 2, D, FF_HALF)
    down_w = w_down.reshape(EXPERTS, 2, FF_HALF, D)
    outputs = lax.map(run_expert, (buffer, gate_w, up_w, down_w))
    picked = outputs[flat.reshape(-1), rowpos.reshape(-1)].reshape(TOKENS, TOP, D).astype(jnp.float32)
    mixed = lax.optimization_barrier(jnp.sum(combine_weights[:, :, None] * picked, axis=1))
    return (stream + mixed).astype(jnp.bfloat16)
```

```python
import functools

import jax
import jax.numpy as jnp
from jax import lax
from jax.experimental import pallas as pl
from jax.experimental.pallas import tpu as pltpu
from jax.sharding import PartitionSpec as P


BF = jnp.bfloat16
F32 = jnp.float32


def up_to(value, unit):
    return -(-value // unit) * unit


def dot_rows(a, b):
    return lax.dot_general(a, b, (((1,), (1,)), ((), ())), preferred_element_type=F32)


def attend(query, cache, draft, length, heads, latent, scale):
    cached = jnp.dot(query, cache, preferred_element_type=F32) * scale
    own = dot_rows(query, draft) * scale
    visible = lax.broadcasted_iota(jnp.int32, cached.shape, 1) < length
    row = lax.broadcasted_iota(jnp.int32, own.shape, 0)
    causal = lax.broadcasted_iota(jnp.int32, own.shape, 1) * heads <= row
    cached = jnp.where(visible, cached, -1e30)
    own = jnp.where(causal, own, -1e30)
    highest = jnp.maximum(
        jnp.max(cached, axis=-1, keepdims=True), jnp.max(own, axis=-1, keepdims=True)
    )
    cached = jnp.exp(cached - highest)
    own = jnp.exp(own - highest)
    total = jnp.sum(cached, axis=-1, keepdims=True) + jnp.sum(own, axis=-1, keepdims=True)
    part = 1.0 / total
    mixed = dot_rows((cached * part).astype(BF), cache[:latent])
    mixed += jnp.dot((own * part).astype(BF), draft[:, :latent], preferred_element_type=F32)
    return mixed.astype(BF).astype(F32)


def tables(routes, weights, meta, slots):
    top, tokens = routes.shape
    planes, qs, lanes = meta.shape
    side = qs // slots
    experts = planes * side
    number = lax.broadcasted_iota(jnp.int32, (experts, tokens), 0)
    member = jnp.zeros((experts, tokens), F32)
    weight = jnp.zeros((experts, tokens), F32)
    for k in range(top):
        named = routes[k : k + 1, :] == number
        member = jnp.where(named, 1.0, member)
        weight = jnp.where(named, weights[k : k + 1, :], weight)
    before = lax.broadcasted_iota(jnp.int32, (tokens, tokens), 0)
    after = lax.broadcasted_iota(jnp.int32, (tokens, tokens), 1)
    earlier = jnp.where(before < after, 1.0, 0.0).astype(BF)
    slot = jnp.dot(member.astype(BF), earlier, preferred_element_type=F32)
    slot = jnp.where(member > 0.5, slot, -1.0)
    high = weight.astype(BF).astype(F32)
    rest = jnp.zeros((experts, lanes - 3 * tokens), F32)
    slot = jnp.concatenate([slot, slot, slot, rest - 1.0], axis=1)
    value = jnp.concatenate([member, high, weight - high, rest], axis=1)
    place = lax.broadcasted_iota(jnp.int32, (slots, lanes), 0).astype(F32)
    for e in range(experts):
        block = jnp.where(slot[e : e + 1] == place, value[e : e + 1], 0.0)
        at = e % side * slots
        meta[e // side, at : at + slots] = block.astype(BF)


def plan(planes):
    if planes == 4:
        order = [[0, 2, 1, 3], [1, 2, 0, 3], [2, 0, 1, 3], [3, 0, 2, 1]]
        route = [
            {0: [1], 1: [2], 2: [3]},
            {1: [0, 2], 2: [3]},
            {2: [3, 1], 1: [0]},
            {3: [1, 2], 1: [0]},
        ]
        early = [[1, 1, 0, 1], [1, 0, 1, 1], [1, 1, 1, 1], [1, 1, 0, 1]]
        steps = (
            "P0 S R2b R3b",
            "R2a P2 R1a R1b",
            "F0 P1 F2 R3a",
            "C2 P3 F1 C1",
            "N2 F3 N1 C3",
            "M2 N3 M1 C0",
            "M3 N0 M0",
        )
        return order, route, early, sum([line.split() for line in steps], [])
    order = [sorted(range(planes), key=lambda s: (abs(s - z), s)) for z in range(planes)]
    route = []
    for s in range(planes):
        hops = {z: [z + 1] for z in range(s, planes - 1)}
        hops.update({z: [z - 1] for z in range(1, s + 1)})
        hops[s] = [z for z in (s + 1, s - 1) if 0 <= z < planes]
        route.append(hops)
    early = [[1] * planes for _ in range(planes)]
    steps = ["P0", "S"]
    for t in range(planes + 2):
        for lag, kind in ((-1, "R"), (-1, "P"), (0, "F"), (0, "C"), (1, "N"), (2, "M")):
            if 0 <= t - lag < planes:
                steps.append(kind + str(t - lag) + "a" * (kind == "R"))
    return order, route, early, steps


def run_steps(script, pick, send_meta, relay, forward, compute, finish, combine):
    table = {"P": pick, "F": forward, "C": compute, "N": finish, "M": combine}
    for step in script:
        if step == "S":
            send_meta()
        elif step[0] == "R":
            relay(int(step[1]), int(step[2:] == "a"))
        else:
            table[step[0]](*[int(v) for v in step[1:]])


def choose(values, index):
    total = 0
    for i, value in enumerate(values):
        total = total + value * lax.div(1, 1 + (index - i) * (index - i))
    return total


def expert_kernel(
    planes,
    side,
    slots,
    lengths,
    routes,
    weights,
    drafts,
    residual,
    gain,
    q_hbm,
    cache_hbm,
    vup_hbm,
    gate_hbm,
    up_hbm,
    down_hbm,
    out,
    q_v,
    cache_v,
    vup,
    mixes,
    stream,
    meta,
    w_gate,
    w_up,
    w_down,
    z_rows,
    z_meta,
    stage,
    rows,
    mine,
    pair_out,
    pair_in,
    back_out,
    back_in,
    part_out,
    part_in,
    total,
    q_sem,
    c_sem,
    v_sem,
    w_sem,
    zr_s,
    zr_r,
    zm_s,
    zm_r,
    ip_s,
    ip_r,
    fw_s,
    fw_r,
    pp_s,
    pp_r,
    rt_s,
    rt_r,
    fn_s,
    fn_r,
):
    tokens, width = stream.shape
    pieces = zr_r.shape[1]
    piece = tokens // pieces
    qs = side * slots
    me = lax.axis_index("ep")
    core = lax.rem(me, 2)
    other = 1 - core
    chip = me // 2
    z = chip // side
    q = lax.rem(chip, side)

    def at(zz, qq, cc):
        return {"ep": (zz * side + qq) * 2 + cc}

    def remote(src, dst, send, recv, device):
        return pltpu.make_async_remote_copy(
            src_ref=src,
            dst_ref=dst,
            send_sem=send,
            recv_sem=recv,
            device_id=device,
            device_id_type=pl.DeviceIdType.MESH,
        )

    near, route, early, script = plan(planes)
    chunk = [z] + [choose([near[i][k] for i in range(planes)], z) for k in range(1, planes)]
    flips = [
        None,
        q + 1 - 2 * lax.rem(q, 2),
        lax.rem(q + 2, 4),
        3 - q,
    ]
    turns = [3, 1, 2][: side - 1]

    reqs, draft_heads, _ = q_v.shape
    fetched = []
    for r in range(reqs):
        pair = [
            pltpu.make_async_copy(q_hbm.at[r], q_v.at[r], q_sem.at[r]),
            pltpu.make_async_copy(cache_hbm.at[r], cache_v.at[r], c_sem.at[r]),
        ]
        for load in pair:
            load.start()
        fetched.append(pair)
    vup_load = pltpu.make_async_copy(vup_hbm, vup, v_sem.at[0])
    vup_load.start()
    loads = [
        pltpu.make_async_copy(gate_hbm.at[0], w_gate, w_sem.at[0]),
        pltpu.make_async_copy(up_hbm.at[0], w_up, w_sem.at[1]),
        pltpu.make_async_copy(down_hbm.at[0], w_down, w_sem.at[2]),
    ]
    for load in loads:
        load.start()

    peers = [at(chunk[k], q, core) for k in range(1, planes)]
    peers += [at(z, flips[j], core) for j in turns]
    peers += [at(z, q, other)]
    barrier = pltpu.get_barrier_semaphore()
    for peer in peers:
        pl.semaphore_signal(
            barrier, inc=1, device_id=peer, device_id_type=pl.DeviceIdType.MESH
        )

    tables(routes, weights, meta, slots)
    heads, latent, head = vup.shape
    scale = (head + q_v.shape[2] - latent) ** (-0.5)
    for r in range(reqs):
        for load in fetched[r]:
            load.wait()
        mixed = attend(q_v[r], cache_v[r], drafts[r], lengths[r], heads, latent, scale)
        for g in range(latent // 128):
            mixes[g, r * draft_heads : (r + 1) * draft_heads] = mixed[
                :, g * 128 : (g + 1) * 128
            ]
    vup_load.wait()
    for h in range(heads):
        value = jnp.concatenate(
            [mixes[g, pl.ds(h, tokens, stride=heads), :] for g in range(latent // 128)], axis=1
        ).astype(BF)
        part = slice(h * head, (h + 1) * head)
        stream[:, part] = residual[:, part].astype(F32) + jnp.dot(
            value, vup[h], preferred_element_type=F32
        )
    value = stream[...]
    level = lax.rsqrt(jnp.mean(value * value, axis=-1, keepdims=True) + 1e-06)
    z_rows[z] = (value * level * gain[...]).astype(BF)
    pl.semaphore_wait(barrier, len(peers))

    sends = []

    def go(copy):
        copy.start()
        sends.append(copy)

    def hop(k, p, way, target, valid):
        s = chunk[k]
        place = z_rows.at[s, p * piece : (p + 1) * piece]
        copy = remote(place, place, zr_s.at[k, way, p], zr_r.at[s, p], at(target, q, core))
        pl.when(valid)(copy.start)

    def fans_of(k):
        return [route[near[i][k]].get(i, []) for i in range(planes)]

    def landed(k, p):
        s = chunk[k]
        place = z_rows.at[s, p * piece : (p + 1) * piece]
        return remote(place, place, zr_s.at[k, 0, p], zr_r.at[s, p], at(s, q, core))

    def onward(k):
        fans = fans_of(k)
        for p in range(pieces):
            if k:
                landed(k, p).wait_recv()
            for way in range(max(len(fan) for fan in fans)):
                valid = choose([int(way < len(fan)) for fan in fans], z)
                target = choose([(fan + [0] * (way + 1))[way] for fan in fans], z)
                hop(k, p, way, target, valid == 1)

    def relay(k, when):
        fans = fans_of(k)
        now = [int(bool(fan) and early[i][k] == when) for i, fan in enumerate(fans)]
        if any(now):
            pl.when(choose(now, z) == 1)(lambda: onward(k))

    def arrive(k):
        leaf = choose([int(not fan) for fan in fans_of(k)], z)

        @pl.when(leaf == 1)
        def _():
            for p in range(pieces):
                landed(k, p).wait_recv()

    onward(0)

    def send_meta():
        for k in range(1, planes):
            zd = chunk[k]
            go(remote(meta.at[zd], z_meta.at[z], zm_s.at[k], zm_r.at[z], at(zd, q, core)))

    def pick(k):
        s = chunk[k]
        if k:
            arrive(k)
            device = at(s, q, core)
            remote(z_meta.at[s], z_meta.at[s], zm_s.at[k], zm_r.at[s], device).wait_recv()
            table, values = z_meta[s], z_rows[s]
        else:
            table, values = meta[z], z_rows[z]
        picked = jnp.dot(table[:, :tokens], values, preferred_element_type=F32).astype(BF)
        stage[k] = picked.reshape(side, slots, width)
        for j in turns:
            go(
                remote(
                    stage.at[k, flips[j]],
                    rows.at[core, s, q],
                    ip_s.at[k, j],
                    ip_r.at[s, j],
                    at(z, flips[j], core),
                )
            )
        rows[core, s, q] = stage[k, q]
        cross(k, 0, q)

    def cross(k, j, qk):
        place = rows.at[core, chunk[k], qk]
        go(remote(place, place, fw_s.at[k, j], fw_r.at[chunk[k], j], at(z, q, other)))

    def forward(k):
        s = chunk[k]
        for j in turns[1:] + turns[:1]:
            landing = rows.at[core, s, flips[j]]
            remote(
                landing, landing, ip_s.at[k, j], ip_r.at[s, j], at(z, flips[j], core)
            ).wait_recv()
            cross(k, j, flips[j])

    def compute(*ks):
        for k in ks:
            s = chunk[k]
            for j in [0] + turns:
                landing = rows.at[other, s, flips[j] if j else q]
                remote(
                    landing, landing, fw_s.at[k, j], fw_r.at[s, j], at(z, q, other)
                ).wait_recv()
        while loads:
            loads.pop(0).wait()
        blocks = [rows[cc, chunk[k]].reshape(qs, width) for cc in (other, core) for k in ks]
        x = jnp.concatenate(blocks, axis=0)
        gate = dot_rows(x, w_gate[...])
        upper = dot_rows(x, w_up[...])
        active = (gate / (1.0 + jnp.exp(-gate)) * upper).astype(BF)
        half = width // 2
        for p in range(2):
            part = slice(p * half, (p + 1) * half)
            both = jnp.dot(active, w_down[:, part], preferred_element_type=F32)
            for i, k in enumerate(ks):
                s = chunk[k]
                pair_out[k, p] = both[i * qs : (i + 1) * qs].astype(BF)
                go(
                    remote(
                        pair_out.at[k, p],
                        pair_in.at[s, p],
                        pp_s.at[k, p],
                        pp_r.at[s, p],
                        at(z, q, other),
                    )
                )
                i += len(ks)
                mine[k, p] = both[i * qs : (i + 1) * qs]

    def finish(k):
        s = chunk[k]
        half = width // 2
        for p in range(2):
            landing = pair_in.at[s, p]
            remote(
                landing, landing, pp_s.at[k, p], pp_r.at[s, p], at(z, q, other)
            ).wait_recv()
            done = (mine[k, p] + pair_in[s, p].astype(F32)).astype(BF)
            back_out[k, :, :, p * half : (p + 1) * half] = done.reshape(side, slots, half)
        for j in turns:
            go(
                remote(
                    back_out.at[k, flips[j]],
                    back_in.at[s, q],
                    rt_s.at[k, j],
                    rt_r.at[s, j],
                    at(z, flips[j], core),
                )
            )
        back_in[s, q] = back_out[k, q]

    def combine(k):
        s = chunk[k]
        for j in turns:
            landing = back_in.at[s, flips[j]]
            remote(
                landing, landing, rt_s.at[k, j], rt_r.at[s, j], at(z, flips[j], core)
            ).wait_recv()
        table = z_meta[s] if k else meta[z]
        weigh = jnp.transpose(table.astype(F32))[tokens : 3 * tokens].astype(BF)
        values = back_in[s].reshape(qs, width)
        both = jnp.dot(weigh, values, preferred_element_type=F32)
        part = both[:tokens] + both[tokens:]
        if k:
            part_out[k] = part.astype(BF)
            go(
                remote(
                    part_out.at[k],
                    part_in.at[z],
                    fn_s.at[k],
                    fn_r.at[z],
                    at(s, q, core),
                )
            )
        else:
            total[...] = stream[...] + part

    run_steps(script, pick, send_meta, relay, forward, compute, finish, combine)

    result = total[...]
    for k in range(1, planes):
        s = chunk[k]
        landing = part_in.at[s]
        remote(landing, landing, fn_s.at[k], fn_r.at[s], at(s, q, core)).wait_recv()
        result = result + part_in[s].astype(F32)
    out[...] = result.astype(BF)
    for copy in sends:
        copy.wait_send()
    for k in range(planes):
        fans = fans_of(k)
        for p in range(pieces):
            for way in range(max(len(fan) for fan in fans)):
                valid = choose([int(way < len(fan)) for fan in fans], z)
                place = z_rows.at[chunk[k], p * piece : (p + 1) * piece]
                copy = remote(place, place, zr_s.at[k, way, p], zr_r.at[z, p], at(z, q, other))
                pl.when(valid == 1)(copy.wait_send)


def local(
    queries,
    cache,
    drafts,
    lengths,
    value_up,
    residual,
    norm_gain,
    w_gate,
    w_up,
    w_down,
    routes,
    combine_weights,
):
    tokens, width = residual.shape
    top = routes.shape[1]
    hidden = w_gate.shape[2]
    reqs, draft, heads, key = queries.shape
    queries = queries.reshape(reqs, draft * heads, key)
    cache = jnp.transpose(cache, (0, 2, 1))
    w_gate = jnp.transpose(w_gate, (0, 2, 1))
    w_up = jnp.transpose(w_up, (0, 2, 1))
    experts = lax.axis_size("ep") // 2
    capacity = min(tokens, 2 * (((tokens * top + experts - 1) // experts + 3) // 2))
    slots = up_to(capacity, 16)
    side = 4 if experts % 4 == 0 else 1
    planes = experts // side
    qs = side * slots
    lanes = up_to(3 * tokens + 1, 128)
    vm = pl.BlockSpec(memory_space=pltpu.VMEM)
    hbm = pl.BlockSpec(memory_space=pl.ANY)
    dma = pltpu.SemaphoreType.DMA
    block = (planes, side, slots, width)
    return pl.pallas_call(
        functools.partial(expert_kernel, planes, side, slots),
        out_shape=jax.ShapeDtypeStruct((tokens, width), BF),
        in_specs=[pl.BlockSpec(memory_space=pltpu.SMEM)] + [vm] * 5 + [hbm] * 6,
        out_specs=vm,
        scratch_shapes=[
            pltpu.VMEM(queries.shape, BF),
            pltpu.VMEM(cache.shape, BF),
            pltpu.VMEM(value_up.shape, BF),
            pltpu.VMEM((value_up.shape[1] // 128, tokens * heads, 128), F32),
            pltpu.VMEM((tokens, width), F32),
            pltpu.VMEM((planes, qs, lanes), BF),
            pltpu.VMEM((hidden, width), BF),
            pltpu.VMEM((hidden, width), BF),
            pltpu.VMEM((hidden, width), BF),
            pltpu.VMEM((planes, tokens, width), BF),
            pltpu.VMEM((planes, qs, lanes), BF),
            pltpu.VMEM(block, BF),
            pltpu.VMEM((2,) + block, BF),
            pltpu.VMEM((planes, 2, qs, width // 2), F32),
            pltpu.VMEM((planes, 2, qs, width // 2), BF),
            pltpu.VMEM((planes, 2, qs, width // 2), BF),
            pltpu.VMEM(block, BF),
            pltpu.VMEM(block, BF),
            pltpu.VMEM((planes, tokens, width), BF),
            pltpu.VMEM((planes, tokens, width), BF),
            pltpu.VMEM((tokens, width), F32),
            dma((reqs,)),
            dma((reqs,)),
            dma((1,)),
            dma((3,)),
        ]
        + [dma((planes, 3, 2)), dma((planes, 2))]
        + [dma((planes,))] * 2
        + [dma((planes, side))] * 4
        + [dma((planes, 2))] * 2
        + [dma((planes, side))] * 2
        + [dma((planes,))] * 2,
        compiler_params=pltpu.CompilerParams(
            collective_id=0, has_side_effects=True, vmem_limit_bytes=60 * 2**20
        ),
    )(
        lengths,
        routes.T,
        combine_weights.T,
        drafts,
        residual,
        norm_gain[None],
        queries,
        cache,
        value_up,
        w_gate,
        w_up,
        w_down,
    )


def solution(mesh):
    placed = (
        P(("groups", "ep"), None, None, None),
        P(("groups", "ep"), None, None),
        P(("groups", "ep"), None, None),
        P(("groups", "ep")),
        P(),
        P(("groups", "ep"), None),
        P(),
        P("ep", None, None),
        P("ep", None, None),
        P("ep", None, None),
        P(("groups", "ep"), None),
        P(("groups", "ep"), None),
    )
    return jax.shard_map(
        local, mesh=mesh, in_specs=placed, out_specs=P(("groups", "ep"), None), check_vma=False
    )
```

```python
import functools

import jax
import jax.numpy as jnp
from jax import lax
from jax.experimental import pallas as pl
from jax.experimental.pallas import tpu as pltpu
from jax.sharding import PartitionSpec as P


BF = jnp.bfloat16
F32 = jnp.float32


def up_to(value, unit):
    return -(-value // unit) * unit


def dot_rows(a, b):
    return lax.dot_general(a, b, (((1,), (1,)), ((), ())), preferred_element_type=F32)


def attend(query, cache, draft, length, heads, latent, scale):
    cached = jnp.dot(query, cache, preferred_element_type=F32) * scale
    own = dot_rows(query, draft) * scale
    visible = lax.broadcasted_iota(jnp.int32, cached.shape, 1) < length
    row = lax.broadcasted_iota(jnp.int32, own.shape, 0)
    causal = lax.broadcasted_iota(jnp.int32, own.shape, 1) * heads <= row
    cached = jnp.where(visible, cached, -1e30)
    own = jnp.where(causal, own, -1e30)
    highest = jnp.maximum(
        jnp.max(cached, axis=-1, keepdims=True), jnp.max(own, axis=-1, keepdims=True)
    )
    cached = jnp.exp(cached - highest)
    own = jnp.exp(own - highest)
    total = jnp.sum(cached, axis=-1, keepdims=True) + jnp.sum(own, axis=-1, keepdims=True)
    part = 1.0 / total
    mixed = dot_rows((cached * part).astype(BF), cache[:latent])
    mixed += jnp.dot((own * part).astype(BF), draft[:, :latent], preferred_element_type=F32)
    return mixed.astype(BF).astype(F32)


def tables(routes, weights, meta, slots):
    top, tokens = routes.shape
    planes, qs, lanes = meta.shape
    side = qs // slots
    experts = planes * side
    number = lax.broadcasted_iota(jnp.int32, (experts, tokens), 0)
    member = jnp.zeros((experts, tokens), F32)
    weight = jnp.zeros((experts, tokens), F32)
    for k in range(top):
        named = routes[k : k + 1, :] == number
        member = jnp.where(named, 1.0, member)
        weight = jnp.where(named, weights[k : k + 1, :], weight)
    before = lax.broadcasted_iota(jnp.int32, (tokens, tokens), 0)
    after = lax.broadcasted_iota(jnp.int32, (tokens, tokens), 1)
    earlier = jnp.where(before < after, 1.0, 0.0).astype(BF)
    slot = jnp.dot(member.astype(BF), earlier, preferred_element_type=F32)
    slot = jnp.where(member > 0.5, slot, -1.0)
    high = weight.astype(BF).astype(F32)
    rest = jnp.zeros((experts, lanes - 3 * tokens), F32)
    slot = jnp.concatenate([slot, slot, slot, rest - 1.0], axis=1)
    value = jnp.concatenate([member, high, weight - high, rest], axis=1)
    place = lax.broadcasted_iota(jnp.int32, (slots, lanes), 0).astype(F32)
    for e in range(experts):
        block = jnp.where(slot[e : e + 1] == place, value[e : e + 1], 0.0)
        at = e % side * slots
        meta[e // side, at : at + slots] = block.astype(BF)


def plan(planes):
    if planes == 4:
        order = [[0, 1, 3, 2], [1, 0, 2, 3], [2, 1, 3, 0], [3, 2, 1, 0]]
        route = [
            {0: [1], 1: [2], 2: [3]},
            {1: [2, 0], 2: [3]},
            {2: [3, 1], 1: [0]},
            {3: [2, 1], 1: [0]},
        ]
        early = [[1, 0, 0, 0], [1, 0, 1, 1], [1, 0, 0, 1], [1, 0, 0, 0]]
        steps = (
            "P0 S R1b R1a",
            "P1 R2a F0 R2b",
            "R3a F1 R3b P3",
            "C1 P2 F3 N1",
            "C3 F2 N3 M1",
            "C2 M3 N2 C0",
            "N0 M2 M0",
        )
        return order, route, early, sum([line.split() for line in steps], [])
    order = [sorted(range(planes), key=lambda s: (abs(s - z), s)) for z in range(planes)]
    route = []
    for s in range(planes):
        hops = {z: [z + 1] for z in range(s, planes - 1)}
        hops.update({z: [z - 1] for z in range(1, s + 1)})
        hops[s] = [z for z in (s + 1, s - 1) if 0 <= z < planes]
        route.append(hops)
    early = [[1] * planes for _ in range(planes)]
    steps = ["P0", "S"]
    for t in range(planes + 2):
        for lag, kind in ((-1, "R"), (-1, "P"), (0, "F"), (0, "C"), (1, "N"), (2, "M")):
            if 0 <= t - lag < planes:
                steps.append(kind + str(t - lag) + "a" * (kind == "R"))
    return order, route, early, steps


def run_steps(script, pick, send_meta, relay, forward, compute, finish, combine):
    table = {"P": pick, "F": forward, "C": compute, "N": finish, "M": combine}
    for step in script:
        if step == "S":
            send_meta()
        elif step[0] == "R":
            relay(int(step[1]), int(step[2:] == "a"))
        else:
            table[step[0]](*[int(v) for v in step[1:]])


def choose(values, index):
    total = 0
    for i, value in enumerate(values):
        total = total + value * lax.div(1, 1 + (index - i) * (index - i))
    return total


def expert_kernel(
    planes,
    side,
    slots,
    lengths,
    routes_hbm,
    weights_hbm,
    drafts_hbm,
    residual_hbm,
    gain_hbm,
    q_hbm,
    cache_hbm,
    vup_hbm,
    gate_hbm,
    up_hbm,
    down_hbm,
    out,
    routes,
    weights,
    drafts,
    residual,
    gain,
    q_v,
    cache_v,
    vup,
    mixes,
    stream,
    meta,
    w_gate,
    w_up,
    w_down,
    z_rows,
    z_meta,
    stage,
    rows,
    mine,
    pair_out,
    pair_in,
    back_out,
    back_in,
    part_out,
    part_in,
    total,
    s_sem,
    q_sem,
    c_sem,
    v_sem,
    w_sem,
    zr_s,
    zr_r,
    zm_s,
    zm_r,
    ip_s,
    ip_r,
    fw_s,
    fw_r,
    pp_s,
    pp_r,
    rt_s,
    rt_r,
    fn_s,
    fn_r,
):
    tokens, width = stream.shape
    pieces = zr_r.shape[1]
    piece = tokens // pieces
    qs = side * slots
    me = lax.axis_index("ep")
    core = lax.rem(me, 2)
    other = 1 - core
    chip = me // 2
    z = chip // side
    q = lax.rem(chip, side)

    def at(zz, qq, cc):
        return {"ep": (zz * side + qq) * 2 + cc}

    def remote(src, dst, send, recv, device):
        return pltpu.make_async_remote_copy(
            src_ref=src,
            dst_ref=dst,
            send_sem=send,
            recv_sem=recv,
            device_id=device,
            device_id_type=pl.DeviceIdType.MESH,
        )

    near, route, early, script = plan(planes)
    chunk = [z] + [choose([near[i][k] for i in range(planes)], z) for k in range(1, planes)]
    flips = [
        None,
        q + 1 - 2 * lax.rem(q, 2),
        lax.rem(q + 2, 4),
        3 - q,
    ]
    turns = [3, 1, 2][: side - 1]

    reqs, draft_heads, _ = q_v.shape
    small = [
        pltpu.make_async_copy(src, dst, s_sem.at[i])
        for i, (src, dst) in enumerate(
            [
                (routes_hbm, routes),
                (weights_hbm, weights),
                (drafts_hbm, drafts),
                (residual_hbm, residual),
                (gain_hbm, gain),
            ]
        )
    ]
    for load in small[:3]:
        load.start()
    fetched = []
    for r in range(reqs):
        pair = [
            pltpu.make_async_copy(q_hbm.at[r], q_v.at[r], q_sem.at[r]),
            pltpu.make_async_copy(cache_hbm.at[r], cache_v.at[r], c_sem.at[r]),
        ]
        for load in pair:
            load.start()
        fetched.append(pair)
    for load in small[3:]:
        load.start()
    vup_load = pltpu.make_async_copy(vup_hbm, vup, v_sem.at[0])
    vup_load.start()
    loads = [
        pltpu.make_async_copy(gate_hbm.at[0], w_gate, w_sem.at[0]),
        pltpu.make_async_copy(up_hbm.at[0], w_up, w_sem.at[1]),
        pltpu.make_async_copy(down_hbm.at[0], w_down, w_sem.at[2]),
    ]
    for load in loads:
        load.start()

    peers = [at(chunk[k], q, core) for k in range(1, planes)]
    peers += [at(z, flips[j], core) for j in turns]
    peers += [at(z, q, other)]
    barrier = pltpu.get_barrier_semaphore()
    for peer in peers:
        pl.semaphore_signal(
            barrier, inc=1, device_id=peer, device_id_type=pl.DeviceIdType.MESH
        )

    for load in small[:3]:
        load.wait()
    tables(routes, weights, meta, slots)
    heads, latent, head = vup.shape
    scale = (head + q_v.shape[2] - latent) ** (-0.5)
    for r in range(reqs):
        for load in fetched[r]:
            load.wait()
        mixed = attend(q_v[r], cache_v[r], drafts[r], lengths[r], heads, latent, scale)
        for g in range(latent // 128):
            mixes[g, r * draft_heads : (r + 1) * draft_heads] = mixed[
                :, g * 128 : (g + 1) * 128
            ]
    for load in small[3:]:
        load.wait()
    vup_load.wait()
    for h in range(heads):
        value = jnp.concatenate(
            [mixes[g, pl.ds(h, tokens, stride=heads), :] for g in range(latent // 128)], axis=1
        ).astype(BF)
        part = slice(h * head, (h + 1) * head)
        stream[:, part] = residual[:, part].astype(F32) + jnp.dot(
            value, vup[h], preferred_element_type=F32
        )
    value = stream[...]
    level = lax.rsqrt(jnp.mean(value * value, axis=-1, keepdims=True) + 1e-06)
    z_rows[z] = (value * level * gain[...]).astype(BF)
    pl.semaphore_wait(barrier, len(peers))

    sends = []

    def go(copy):
        copy.start()
        sends.append(copy)

    def hop(k, p, way, target, valid):
        s = chunk[k]
        place = z_rows.at[s, p * piece : (p + 1) * piece]
        copy = remote(place, place, zr_s.at[k, way, p], zr_r.at[s, p], at(target, q, core))
        pl.when(valid)(copy.start)

    def fans_of(k):
        return [route[near[i][k]].get(i, []) for i in range(planes)]

    def landed(k, p):
        s = chunk[k]
        place = z_rows.at[s, p * piece : (p + 1) * piece]
        return remote(place, place, zr_s.at[k, 0, p], zr_r.at[s, p], at(s, q, core))

    def onward(k):
        fans = fans_of(k)
        for p in range(pieces):
            if k:
                landed(k, p).wait_recv()
            for way in range(max(len(fan) for fan in fans)):
                valid = choose([int(way < len(fan)) for fan in fans], z)
                target = choose([(fan + [0] * (way + 1))[way] for fan in fans], z)
                hop(k, p, way, target, valid == 1)

    def relay(k, when):
        fans = fans_of(k)
        now = [int(bool(fan) and early[i][k] == when) for i, fan in enumerate(fans)]
        if any(now):
            pl.when(choose(now, z) == 1)(lambda: onward(k))

    def arrive(k):
        leaf = choose([int(not fan) for fan in fans_of(k)], z)

        @pl.when(leaf == 1)
        def _():
            for p in range(pieces):
                landed(k, p).wait_recv()

    onward(0)

    def send_meta():
        for k in range(1, planes):
            zd = chunk[k]
            go(remote(meta.at[zd], z_meta.at[z], zm_s.at[k], zm_r.at[z], at(zd, q, core)))

    def pick(k):
        s = chunk[k]
        if k:
            arrive(k)
            device = at(s, q, core)
            remote(z_meta.at[s], z_meta.at[s], zm_s.at[k], zm_r.at[s], device).wait_recv()
            table, values = z_meta[s], z_rows[s]
        else:
            table, values = meta[z], z_rows[z]
        picked = jnp.dot(table[:, :tokens], values, preferred_element_type=F32).astype(BF)
        stage[k] = picked.reshape(side, slots, width)
        for j in turns:
            go(
                remote(
                    stage.at[k, flips[j]],
                    rows.at[core, s, q],
                    ip_s.at[k, j],
                    ip_r.at[s, j],
                    at(z, flips[j], core),
                )
            )
        rows[core, s, q] = stage[k, q]
        cross(k, 0, q)

    def cross(k, j, qk):
        place = rows.at[core, chunk[k], qk]
        go(remote(place, place, fw_s.at[k, j], fw_r.at[chunk[k], j], at(z, q, other)))

    def forward(k):
        s = chunk[k]
        for j in turns[1:] + turns[:1]:
            landing = rows.at[core, s, flips[j]]
            remote(
                landing, landing, ip_s.at[k, j], ip_r.at[s, j], at(z, flips[j], core)
            ).wait_recv()
            cross(k, j, flips[j])

    def compute(*ks):
        for k in ks:
            s = chunk[k]
            for j in [0] + turns:
                landing = rows.at[other, s, flips[j] if j else q]
                remote(
                    landing, landing, fw_s.at[k, j], fw_r.at[s, j], at(z, q, other)
                ).wait_recv()
        while loads:
            loads.pop(0).wait()
        blocks = [rows[cc, chunk[k]].reshape(qs, width) for cc in (other, core) for k in ks]
        x = jnp.concatenate(blocks, axis=0)
        gate = dot_rows(x, w_gate[...])
        upper = dot_rows(x, w_up[...])
        active = (gate / (1.0 + jnp.exp(-gate)) * upper).astype(BF)
        half = width // 2
        for p in range(2):
            part = slice(p * half, (p + 1) * half)
            both = jnp.dot(active, w_down[:, part], preferred_element_type=F32)
            for i, k in enumerate(ks):
                s = chunk[k]
                pair_out[k, p] = both[i * qs : (i + 1) * qs].astype(BF)
                go(
                    remote(
                        pair_out.at[k, p],
                        pair_in.at[s, p],
                        pp_s.at[k, p],
                        pp_r.at[s, p],
                        at(z, q, other),
                    )
                )
                i += len(ks)
                mine[k, p] = both[i * qs : (i + 1) * qs]

    def finish(k):
        s = chunk[k]
        half = width // 2
        for p in range(2):
            landing = pair_in.at[s, p]
            remote(
                landing, landing, pp_s.at[k, p], pp_r.at[s, p], at(z, q, other)
            ).wait_recv()
            done = (mine[k, p] + pair_in[s, p].astype(F32)).astype(BF)
            back_out[k, :, :, p * half : (p + 1) * half] = done.reshape(side, slots, half)
        for j in turns:
            go(
                remote(
                    back_out.at[k, flips[j]],
                    back_in.at[s, q],
                    rt_s.at[k, j],
                    rt_r.at[s, j],
                    at(z, flips[j], core),
                )
            )
        back_in[s, q] = back_out[k, q]

    def combine(k):
        s = chunk[k]
        for j in turns:
            landing = back_in.at[s, flips[j]]
            remote(
                landing, landing, rt_s.at[k, j], rt_r.at[s, j], at(z, flips[j], core)
            ).wait_recv()
        table = z_meta[s] if k else meta[z]
        weigh = jnp.transpose(table.astype(F32))[tokens : 3 * tokens].astype(BF)
        values = back_in[s].reshape(qs, width)
        both = jnp.dot(weigh, values, preferred_element_type=F32)
        part = both[:tokens] + both[tokens:]
        if k:
            part_out[k] = part.astype(BF)
            go(
                remote(
                    part_out.at[k],
                    part_in.at[z],
                    fn_s.at[k],
                    fn_r.at[z],
                    at(s, q, core),
                )
            )
        else:
            total[...] = stream[...] + part

    run_steps(script, pick, send_meta, relay, forward, compute, finish, combine)

    result = total[...]
    for k in range(1, planes):
        s = chunk[k]
        landing = part_in.at[s]
        remote(landing, landing, fn_s.at[k], fn_r.at[s], at(s, q, core)).wait_recv()
        result = result + part_in[s].astype(F32)
    out[...] = result.astype(BF)
    for copy in sends:
        copy.wait_send()
    for k in range(planes):
        fans = fans_of(k)
        for p in range(pieces):
            for way in range(max(len(fan) for fan in fans)):
                valid = choose([int(way < len(fan)) for fan in fans], z)
                place = z_rows.at[chunk[k], p * piece : (p + 1) * piece]
                copy = remote(place, place, zr_s.at[k, way, p], zr_r.at[z, p], at(z, q, other))
                pl.when(valid == 1)(copy.wait_send)


def local(
    queries,
    cache,
    drafts,
    lengths,
    value_up,
    residual,
    norm_gain,
    w_gate,
    w_up,
    w_down,
    routes,
    combine_weights,
):
    tokens, width = residual.shape
    top = routes.shape[1]
    hidden = w_gate.shape[2]
    reqs, draft, heads, key = queries.shape
    queries = queries.reshape(reqs, draft * heads, key)
    cache = jnp.transpose(cache, (0, 2, 1))
    w_gate = jnp.transpose(w_gate, (0, 2, 1))
    w_up = jnp.transpose(w_up, (0, 2, 1))
    experts = lax.axis_size("ep") // 2
    capacity = min(tokens, 2 * (((tokens * top + experts - 1) // experts + 3) // 2))
    slots = up_to(capacity, 16)
    side = 4 if experts % 4 == 0 else 1
    planes = experts // side
    qs = side * slots
    lanes = up_to(3 * tokens + 1, 128)
    vm = pl.BlockSpec(memory_space=pltpu.VMEM)
    hbm = pl.BlockSpec(memory_space=pl.ANY)
    dma = pltpu.SemaphoreType.DMA
    block = (planes, side, slots, width)
    return pl.pallas_call(
        functools.partial(expert_kernel, planes, side, slots),
        out_shape=pltpu.VMEM((tokens, width), BF),
        in_specs=[pl.BlockSpec(memory_space=pltpu.SMEM)] + [hbm] * 11,
        out_specs=vm,
        scratch_shapes=[
            pltpu.VMEM((routes.shape[1], tokens), routes.dtype),
            pltpu.VMEM((routes.shape[1], tokens), F32),
            pltpu.VMEM(drafts.shape, BF),
            pltpu.VMEM(residual.shape, BF),
            pltpu.VMEM((1, width), F32),
            pltpu.VMEM(queries.shape, BF),
            pltpu.VMEM(cache.shape, BF),
            pltpu.VMEM(value_up.shape, BF),
            pltpu.VMEM((value_up.shape[1] // 128, tokens * heads, 128), F32),
            pltpu.VMEM((tokens, width), F32),
            pltpu.VMEM((planes, qs, lanes), BF),
            pltpu.VMEM((hidden, width), BF),
            pltpu.VMEM((hidden, width), BF),
            pltpu.VMEM((hidden, width), BF),
            pltpu.VMEM((planes, tokens, width), BF),
            pltpu.VMEM((planes, qs, lanes), BF),
            pltpu.VMEM(block, BF),
            pltpu.VMEM((2,) + block, BF),
            pltpu.VMEM((planes, 2, qs, width // 2), F32),
            pltpu.VMEM((planes, 2, qs, width // 2), BF),
            pltpu.VMEM((planes, 2, qs, width // 2), BF),
            pltpu.VMEM(block, BF),
            pltpu.VMEM(block, BF),
            pltpu.VMEM((planes, tokens, width), BF),
            pltpu.VMEM((planes, tokens, width), BF),
            pltpu.VMEM((tokens, width), F32),
            dma((5,)),
            dma((reqs,)),
            dma((reqs,)),
            dma((1,)),
            dma((3,)),
        ]
        + [dma((planes, 3, 2)), dma((planes, 2))]
        + [dma((planes,))] * 2
        + [dma((planes, side))] * 4
        + [dma((planes, 2))] * 2
        + [dma((planes, side))] * 2
        + [dma((planes,))] * 2,
        compiler_params=pltpu.CompilerParams(
            collective_id=0, has_side_effects=True, vmem_limit_bytes=60 * 2**20
        ),
    )(
        lengths,
        routes.T,
        combine_weights.T,
        drafts,
        residual,
        norm_gain[None],
        queries,
        cache,
        value_up,
        w_gate,
        w_up,
        w_down,
    )


def solution(mesh):
    placed = (
        P(("groups", "ep"), None, None, None),
        P(("groups", "ep"), None, None),
        P(("groups", "ep"), None, None),
        P(("groups", "ep")),
        P(),
        P(("groups", "ep"), None),
        P(),
        P("ep", None, None),
        P("ep", None, None),
        P("ep", None, None),
        P(("groups", "ep"), None),
        P(("groups", "ep"), None),
    )
    return jax.shard_map(
        local, mesh=mesh, in_specs=placed, out_specs=P(("groups", "ep"), None), check_vma=False
    )
```

```python
import functools

import jax
import jax.numpy as jnp
from jax import lax
from jax.experimental import pallas as pl
from jax.experimental.pallas import tpu as pltpu
from jax.sharding import PartitionSpec as P


BF = jnp.bfloat16
F32 = jnp.float32


def up_to(value, unit):
    return -(-value // unit) * unit


def dot_rows(a, b):
    return lax.dot_general(a, b, (((1,), (1,)), ((), ())), preferred_element_type=F32)


def attend(query, cache, draft, length, heads, latent, scale):
    cached = jnp.dot(query, cache, preferred_element_type=F32) * scale
    own = dot_rows(query, draft) * scale
    visible = lax.broadcasted_iota(jnp.int32, cached.shape, 1) < length
    row = lax.broadcasted_iota(jnp.int32, own.shape, 0)
    causal = lax.broadcasted_iota(jnp.int32, own.shape, 1) * heads <= row
    cached = jnp.where(visible, cached, -1e30)
    own = jnp.where(causal, own, -1e30)
    highest = jnp.maximum(
        jnp.max(cached, axis=-1, keepdims=True), jnp.max(own, axis=-1, keepdims=True)
    )
    cached = jnp.exp(cached - highest)
    own = jnp.exp(own - highest)
    total = jnp.sum(cached, axis=-1, keepdims=True) + jnp.sum(own, axis=-1, keepdims=True)
    part = 1.0 / total
    mixed = dot_rows((cached * part).astype(BF), cache[:latent])
    mixed += jnp.dot((own * part).astype(BF), draft[:, :latent], preferred_element_type=F32)
    return mixed.astype(BF).astype(F32)


def tables(routes, weights, meta, slots):
    top, tokens = routes.shape
    planes, qs, lanes = meta.shape
    side = qs // slots
    experts = planes * side
    number = lax.broadcasted_iota(jnp.int32, (experts, tokens), 0)
    member = jnp.zeros((experts, tokens), F32)
    weight = jnp.zeros((experts, tokens), F32)
    for k in range(top):
        named = routes[k : k + 1, :] == number
        member = jnp.where(named, 1.0, member)
        weight = jnp.where(named, weights[k : k + 1, :], weight)
    before = lax.broadcasted_iota(jnp.int32, (tokens, tokens), 0)
    after = lax.broadcasted_iota(jnp.int32, (tokens, tokens), 1)
    earlier = jnp.where(before < after, 1.0, 0.0).astype(BF)
    slot = jnp.dot(member.astype(BF), earlier, preferred_element_type=F32)
    slot = jnp.where(member > 0.5, slot, -1.0)
    high = weight.astype(BF).astype(F32)
    rest = jnp.zeros((experts, lanes - 3 * tokens), F32)
    slot = jnp.concatenate([slot, slot, slot, rest - 1.0], axis=1)
    value = jnp.concatenate([member, high, weight - high, rest], axis=1)
    place = lax.broadcasted_iota(jnp.int32, (slots, lanes), 0).astype(F32)
    for e in range(experts):
        block = jnp.where(slot[e : e + 1] == place, value[e : e + 1], 0.0)
        at = e % side * slots
        meta[e // side, at : at + slots] = block.astype(BF)


def plan(planes):
    if planes == 4:
        order = [[0, 1, 3, 2], [1, 0, 2, 3], [2, 1, 3, 0], [3, 2, 1, 0]]
        route = [
            {0: [1], 1: [2], 2: [3]},
            {1: [2, 0], 2: [3]},
            {2: [3, 1], 1: [0]},
            {3: [2, 1], 1: [0]},
        ]
        early = [[1, 0, 0, 0], [1, 0, 1, 0], [1, 0, 0, 1], [1, 0, 0, 0]]
        steps = (
            "P0 S R1b R1a",
            "P1 F0 R2b R2a",
            "R3a F1 R3b P3",
            "C1 P2 F3 N1",
            "C3 F2 N3 M1",
            "C20 M3 N2 N0",
            "M2 M0",
        )
        return order, route, early, sum([line.split() for line in steps], [])
    order = [sorted(range(planes), key=lambda s: (abs(s - z), s)) for z in range(planes)]
    route = []
    for s in range(planes):
        hops = {z: [z + 1] for z in range(s, planes - 1)}
        hops.update({z: [z - 1] for z in range(1, s + 1)})
        hops[s] = [z for z in (s + 1, s - 1) if 0 <= z < planes]
        route.append(hops)
    early = [[1] * planes for _ in range(planes)]
    steps = ["P0", "S"]
    for t in range(planes + 2):
        for lag, kind in ((-1, "R"), (-1, "P"), (0, "F"), (0, "C"), (1, "N"), (2, "M")):
            if 0 <= t - lag < planes:
                steps.append(kind + str(t - lag) + "a" * (kind == "R"))
    return order, route, early, steps


def run_steps(script, pick, send_meta, relay, forward, compute, finish, combine):
    table = {"P": pick, "F": forward, "C": compute, "N": finish, "M": combine}
    for step in script:
        if step == "S":
            send_meta()
        elif step[0] == "R":
            relay(int(step[1]), int(step[2:] == "a"))
        else:
            table[step[0]](*[int(v) for v in step[1:]])


def choose(values, index):
    total = 0
    for i, value in enumerate(values):
        total = total + value * lax.div(1, 1 + (index - i) * (index - i))
    return total


def expert_kernel(
    planes,
    side,
    slots,
    lengths_hbm,
    routes_hbm,
    weights_hbm,
    drafts_hbm,
    residual_hbm,
    gain_hbm,
    q_hbm,
    cache_hbm,
    vup_hbm,
    gate_hbm,
    up_hbm,
    down_hbm,
    out,
    lengths,
    routes,
    weights,
    drafts,
    residual,
    gain,
    q_v,
    cache_v,
    vup,
    mixes,
    stream,
    meta,
    w_gate,
    w_up,
    w_down,
    z_rows,
    z_meta,
    stage,
    rows,
    mine,
    pair_out,
    pair_in,
    back_out,
    back_in,
    part_out,
    part_in,
    total,
    far_sem,
    s_sem,
    q_sem,
    c_sem,
    v_sem,
    w_sem,
    zr_s,
    zr_r,
    zm_s,
    zm_r,
    ip_s,
    ip_r,
    fw_s,
    fw_r,
    pp_s,
    pp_r,
    rt_s,
    rt_r,
    fn_s,
    fn_r,
):
    tokens, width = stream.shape
    pieces = zr_r.shape[1]
    piece = tokens // pieces
    qs = side * slots
    me = lax.axis_index("ep")
    core = lax.rem(me, 2)
    other = 1 - core
    chip = me // 2
    z = chip // side
    q = lax.rem(chip, side)

    def at(zz, qq, cc):
        return {"ep": (zz * side + qq) * 2 + cc}

    def remote(src, dst, send, recv, device):
        return pltpu.make_async_remote_copy(
            src_ref=src,
            dst_ref=dst,
            send_sem=send,
            recv_sem=recv,
            device_id=device,
            device_id_type=pl.DeviceIdType.MESH,
        )

    near, route, early, script = plan(planes)
    chunk = [z] + [choose([near[i][k] for i in range(planes)], z) for k in range(1, planes)]
    flips = [
        None,
        q + 1 - 2 * lax.rem(q, 2),
        lax.rem(q + 2, 4),
        3 - q,
    ]
    turns = [3, 1, 2][: side - 1]

    reqs, draft_heads, _ = q_v.shape
    small = [
        pltpu.make_async_copy(src, dst, s_sem.at[i])
        for i, (src, dst) in enumerate(
            [
                (routes_hbm, routes),
                (weights_hbm, weights),
                (drafts_hbm, drafts),
                (residual_hbm, residual),
                (gain_hbm, gain),
                (lengths_hbm, lengths),
            ]
        )
    ]
    for load in small[2:3] + small[5:]:
        load.start()
    fetched = []
    for r in range(reqs):
        pair = [
            pltpu.make_async_copy(q_hbm.at[r], q_v.at[r], q_sem.at[r]),
            pltpu.make_async_copy(cache_hbm.at[r], cache_v.at[r], c_sem.at[r]),
        ]
        for load in pair:
            load.start()
        fetched.append(pair)
    for load in small[:2] + small[3:5]:
        load.start()
    vup_load = pltpu.make_async_copy(vup_hbm, vup, v_sem.at[0])
    vup_load.start()
    loads = [
        pltpu.make_async_copy(gate_hbm.at[0], w_gate, w_sem.at[0]),
        pltpu.make_async_copy(up_hbm.at[0], w_up, w_sem.at[1]),
        pltpu.make_async_copy(down_hbm.at[0], w_down, w_sem.at[2]),
    ]
    for load in loads:
        load.start()

    def flag(test, k):
        return choose([int(test(i, near[i][k])) for i in range(planes)], z) == 1

    def signal(semaphore, device):
        pl.semaphore_signal(
            semaphore, inc=1, device_id=device, device_id_type=pl.DeviceIdType.MESH
        )

    barrier = pltpu.get_barrier_semaphore()
    for j in turns:
        signal(barrier, at(z, flips[j], core))
    signal(barrier, at(z, q, other))
    for k in range(1, planes):
        pl.when(flag(lambda i, d: d >= i - 1, k))(
            functools.partial(signal, barrier, at(chunk[k], q, core))
        )
    heard = [sum(s != i and s <= i + 1 for s in range(planes)) for i in range(planes)]

    for load in small[2:3] + small[5:]:
        load.wait()
    heads, latent, head = vup.shape
    scale = (head + q_v.shape[2] - latent) ** (-0.5)
    for r in range(reqs):
        if r == reqs - 1:
            pl.semaphore_wait(barrier, len(turns) + 1 + choose(heard, z))
            for k in range(1, planes):
                pl.when(flag(lambda i, d: d < i - 1, k))(
                    functools.partial(signal, far_sem.at[z], at(chunk[k], q, core))
                )
        for load in fetched[r]:
            load.wait()
        mixed = attend(q_v[r], cache_v[r], drafts[r], lengths[:, r : r + 1], heads, latent, scale)
        for g in range(latent // 128):
            mixes[g, r * draft_heads : (r + 1) * draft_heads] = mixed[
                :, g * 128 : (g + 1) * 128
            ]
    for load in small[:2] + small[3:5]:
        load.wait()
    tables(routes, weights, meta, slots)
    vup_load.wait()
    for h in range(heads):
        value = jnp.concatenate(
            [mixes[g, pl.ds(h, tokens, stride=heads), :] for g in range(latent // 128)], axis=1
        ).astype(BF)
        part = slice(h * head, (h + 1) * head)
        stream[:, part] = residual[:, part].astype(F32) + jnp.dot(
            value, vup[h], preferred_element_type=F32
        )
    value = stream[...]
    level = lax.rsqrt(jnp.mean(value * value, axis=-1, keepdims=True) + 1e-06)
    z_rows[z] = (value * level * gain[...]).astype(BF)
    sends = []

    def go(copy):
        copy.start()
        sends.append(copy)

    def hop(k, p, way, target, valid):
        s = chunk[k]
        place = z_rows.at[s, p * piece : (p + 1) * piece]
        copy = remote(place, place, zr_s.at[k, way, p], zr_r.at[s, p], at(target, q, core))
        pl.when(valid)(copy.start)

    def fans_of(k):
        return [route[near[i][k]].get(i, []) for i in range(planes)]

    def landed(k, p):
        s = chunk[k]
        place = z_rows.at[s, p * piece : (p + 1) * piece]
        return remote(place, place, zr_s.at[k, 0, p], zr_r.at[s, p], at(s, q, core))

    def onward(k):
        fans = fans_of(k)
        for p in range(pieces):
            if k:
                landed(k, p).wait_recv()
            for way in range(max(len(fan) for fan in fans)):
                valid = choose([int(way < len(fan)) for fan in fans], z)
                target = choose([(fan + [0] * (way + 1))[way] for fan in fans], z)
                hop(k, p, way, target, valid == 1)

    def relay(k, when):
        fans = fans_of(k)
        now = [int(bool(fan) and early[i][k] == when) for i, fan in enumerate(fans)]
        if any(now):
            pl.when(choose(now, z) == 1)(lambda: onward(k))

    def arrive(k):
        leaf = choose([int(not fan) for fan in fans_of(k)], z)

        @pl.when(leaf == 1)
        def _():
            for p in range(pieces):
                landed(k, p).wait_recv()

    onward(0)

    def send_meta():
        for k in range(1, planes):
            zd = chunk[k]
            pl.when(flag(lambda i, d: d > i + 1, k))(
                functools.partial(pl.semaphore_wait, far_sem.at[zd], 1)
            )
            go(remote(meta.at[zd], z_meta.at[z], zm_s.at[k], zm_r.at[z], at(zd, q, core)))

    def pick(k):
        s = chunk[k]
        if k:
            arrive(k)
            device = at(s, q, core)
            remote(z_meta.at[s], z_meta.at[s], zm_s.at[k], zm_r.at[s], device).wait_recv()
            table, values = z_meta[s], z_rows[s]
        else:
            table, values = meta[z], z_rows[z]
        picked = jnp.dot(table[:, :tokens], values, preferred_element_type=F32).astype(BF)
        stage[k] = picked.reshape(side, slots, width)
        for j in turns:
            go(
                remote(
                    stage.at[k, flips[j]],
                    rows.at[core, s, q],
                    ip_s.at[k, j],
                    ip_r.at[s, j],
                    at(z, flips[j], core),
                )
            )
        rows[core, s, q] = stage[k, q]
        cross(k, 0, q)

    def cross(k, j, qk):
        place = rows.at[core, chunk[k], qk]
        go(remote(place, place, fw_s.at[k, j], fw_r.at[chunk[k], j], at(z, q, other)))

    def forward(k):
        s = chunk[k]
        for j in turns[1:] + turns[:1]:
            landing = rows.at[core, s, flips[j]]
            remote(
                landing, landing, ip_s.at[k, j], ip_r.at[s, j], at(z, flips[j], core)
            ).wait_recv()
            cross(k, j, flips[j])

    def compute(*ks):
        for k in ks:
            s = chunk[k]
            for j in [0] + turns:
                landing = rows.at[other, s, flips[j] if j else q]
                remote(
                    landing, landing, fw_s.at[k, j], fw_r.at[s, j], at(z, q, other)
                ).wait_recv()
        while loads:
            loads.pop(0).wait()
        blocks = [rows[cc, chunk[k]].reshape(qs, width) for cc in (other, core) for k in ks]
        x = jnp.concatenate(blocks, axis=0)
        gate = dot_rows(x, w_gate[...])
        upper = dot_rows(x, w_up[...])
        active = (gate / (1.0 + jnp.exp(-gate)) * upper).astype(BF)
        half = width // 2
        for p in range(2):
            part = slice(p * half, (p + 1) * half)
            both = jnp.dot(active, w_down[:, part], preferred_element_type=F32)
            for i, k in enumerate(ks):
                s = chunk[k]
                pair_out[k, p] = both[i * qs : (i + 1) * qs].astype(BF)
                go(
                    remote(
                        pair_out.at[k, p],
                        pair_in.at[s, p],
                        pp_s.at[k, p],
                        pp_r.at[s, p],
                        at(z, q, other),
                    )
                )
                i += len(ks)
                mine[k, p] = both[i * qs : (i + 1) * qs]

    def finish(k):
        s = chunk[k]
        half = width // 2
        for p in range(2):
            landing = pair_in.at[s, p]
            remote(
                landing, landing, pp_s.at[k, p], pp_r.at[s, p], at(z, q, other)
            ).wait_recv()
            done = (mine[k, p] + pair_in[s, p].astype(F32)).astype(BF)
            back_out[k, :, :, p * half : (p + 1) * half] = done.reshape(side, slots, half)
        for j in turns:
            go(
                remote(
                    back_out.at[k, flips[j]],
                    back_in.at[s, q],
                    rt_s.at[k, j],
                    rt_r.at[s, j],
                    at(z, flips[j], core),
                )
            )
        back_in[s, q] = back_out[k, q]

    def combine(k):
        s = chunk[k]
        for j in turns:
            landing = back_in.at[s, flips[j]]
            remote(
                landing, landing, rt_s.at[k, j], rt_r.at[s, j], at(z, flips[j], core)
            ).wait_recv()
        table = z_meta[s] if k else meta[z]
        weigh = jnp.transpose(table.astype(F32))[tokens : 3 * tokens].astype(BF)
        values = back_in[s].reshape(qs, width)
        both = jnp.dot(weigh, values, preferred_element_type=F32)
        part = both[:tokens] + both[tokens:]
        if k:
            part_out[k] = part.astype(BF)
            go(
                remote(
                    part_out.at[k],
                    part_in.at[z],
                    fn_s.at[k],
                    fn_r.at[z],
                    at(s, q, core),
                )
            )
        else:
            total[...] = stream[...] + part

    run_steps(script, pick, send_meta, relay, forward, compute, finish, combine)

    result = total[...]
    for k in range(1, planes):
        s = chunk[k]
        landing = part_in.at[s]
        remote(landing, landing, fn_s.at[k], fn_r.at[s], at(s, q, core)).wait_recv()
        result = result + part_in[s].astype(F32)
    out[...] = result.astype(BF)
    for copy in sends:
        copy.wait_send()
    for k in range(planes):
        fans = fans_of(k)
        for p in range(pieces):
            for way in range(max(len(fan) for fan in fans)):
                valid = choose([int(way < len(fan)) for fan in fans], z)
                place = z_rows.at[chunk[k], p * piece : (p + 1) * piece]
                copy = remote(place, place, zr_s.at[k, way, p], zr_r.at[z, p], at(z, q, other))
                pl.when(valid == 1)(copy.wait_send)


def local(
    queries,
    cache,
    drafts,
    lengths,
    value_up,
    residual,
    norm_gain,
    w_gate,
    w_up,
    w_down,
    routes,
    combine_weights,
):
    tokens, width = residual.shape
    top = routes.shape[1]
    hidden = w_gate.shape[2]
    reqs, draft, heads, key = queries.shape
    queries = queries.reshape(reqs, draft * heads, key)
    cache = jnp.transpose(cache, (0, 2, 1))
    w_gate = jnp.transpose(w_gate, (0, 2, 1))
    w_up = jnp.transpose(w_up, (0, 2, 1))
    experts = lax.axis_size("ep") // 2
    capacity = min(tokens, 2 * (((tokens * top + experts - 1) // experts + 3) // 2))
    slots = up_to(capacity, 16)
    side = 4 if experts % 4 == 0 else 1
    planes = experts // side
    qs = side * slots
    lanes = up_to(3 * tokens + 1, 128)
    vm = pl.BlockSpec(memory_space=pltpu.VMEM)
    hbm = pl.BlockSpec(memory_space=pl.ANY)
    dma = pltpu.SemaphoreType.DMA
    block = (planes, side, slots, width)
    return pl.pallas_call(
        functools.partial(expert_kernel, planes, side, slots),
        out_shape=pltpu.VMEM((tokens, width), BF),
        in_specs=[hbm] * 12,
        out_specs=vm,
        scratch_shapes=[
            pltpu.VMEM((1, reqs), lengths.dtype),
            pltpu.VMEM((routes.shape[1], tokens), routes.dtype),
            pltpu.VMEM((routes.shape[1], tokens), F32),
            pltpu.VMEM(drafts.shape, BF),
            pltpu.VMEM(residual.shape, BF),
            pltpu.VMEM((1, width), F32),
            pltpu.VMEM(queries.shape, BF),
            pltpu.VMEM(cache.shape, BF),
            pltpu.VMEM(value_up.shape, BF),
            pltpu.VMEM((value_up.shape[1] // 128, tokens * heads, 128), F32),
            pltpu.VMEM((tokens, width), F32),
            pltpu.VMEM((planes, qs, lanes), BF),
            pltpu.VMEM((hidden, width), BF),
            pltpu.VMEM((hidden, width), BF),
            pltpu.VMEM((hidden, width), BF),
            pltpu.VMEM((planes, tokens, width), BF),
            pltpu.VMEM((planes, qs, lanes), BF),
            pltpu.VMEM(block, BF),
            pltpu.VMEM((2,) + block, BF),
            pltpu.VMEM((planes, 2, qs, width // 2), F32),
            pltpu.VMEM((planes, 2, qs, width // 2), BF),
            pltpu.VMEM((planes, 2, qs, width // 2), BF),
            pltpu.VMEM(block, BF),
            pltpu.VMEM(block, BF),
            pltpu.VMEM((planes, tokens, width), BF),
            pltpu.VMEM((planes, tokens, width), BF),
            pltpu.VMEM((tokens, width), F32),
            pltpu.SemaphoreType.REGULAR((planes,)),
            dma((6,)),
            dma((reqs,)),
            dma((reqs,)),
            dma((1,)),
            dma((3,)),
        ]
        + [dma((planes, 3, 1)), dma((planes, 1))]
        + [dma((planes,))] * 2
        + [dma((planes, side))] * 4
        + [dma((planes, 2))] * 2
        + [dma((planes, side))] * 2
        + [dma((planes,))] * 2,
        compiler_params=pltpu.CompilerParams(
            collective_id=0, has_side_effects=True, vmem_limit_bytes=60 * 2**20
        ),
    )(
        lengths[None],
        routes.T,
        combine_weights.T,
        drafts,
        residual,
        norm_gain[None],
        queries,
        cache,
        value_up,
        w_gate,
        w_up,
        w_down,
    )


def solution(mesh):
    placed = (
        P(("groups", "ep"), None, None, None),
        P(("groups", "ep"), None, None),
        P(("groups", "ep"), None, None),
        P(("groups", "ep")),
        P(),
        P(("groups", "ep"), None),
        P(),
        P("ep", None, None),
        P("ep", None, None),
        P("ep", None, None),
        P(("groups", "ep"), None),
        P(("groups", "ep"), None),
    )
    return jax.shard_map(
        local, mesh=mesh, in_specs=placed, out_specs=P(("groups", "ep"), None), check_vma=False
    )
```

```python
import functools

import jax
import jax.numpy as jnp
from jax import lax
from jax.experimental import pallas as pl
from jax.experimental.pallas import tpu as pltpu
from jax.sharding import PartitionSpec as P


BF = jnp.bfloat16
F32 = jnp.float32


def up_to(value, unit):
    return -(-value // unit) * unit


def dot_rows(a, b):
    return lax.dot_general(a, b, (((1,), (1,)), ((), ())), preferred_element_type=F32)


def attend(query, cache, draft, length, heads, latent, scale):
    cached = jnp.dot(query, cache, preferred_element_type=F32) * scale
    own = dot_rows(query, draft) * scale
    visible = lax.broadcasted_iota(jnp.int32, cached.shape, 1) < length
    row = lax.broadcasted_iota(jnp.int32, own.shape, 0)
    causal = lax.broadcasted_iota(jnp.int32, own.shape, 1) * heads <= row
    cached = jnp.where(visible, cached, -1e30)
    own = jnp.where(causal, own, -1e30)
    highest = jnp.maximum(
        jnp.max(cached, axis=-1, keepdims=True), jnp.max(own, axis=-1, keepdims=True)
    )
    cached = jnp.exp(cached - highest)
    own = jnp.exp(own - highest)
    total = jnp.sum(cached, axis=-1, keepdims=True) + jnp.sum(own, axis=-1, keepdims=True)
    part = 1.0 / total
    mixed = dot_rows((cached * part).astype(BF), cache[:latent])
    mixed += jnp.dot((own * part).astype(BF), draft[:, :latent], preferred_element_type=F32)
    return mixed.astype(BF).astype(F32)


def tables(routes, weights, meta, slots):
    top, tokens = routes.shape
    planes, qs, lanes = meta.shape
    side = qs // slots
    experts = planes * side
    number = lax.broadcasted_iota(jnp.int32, (experts, tokens), 0)
    member = jnp.zeros((experts, tokens), F32)
    weight = jnp.zeros((experts, tokens), F32)
    for k in range(top):
        named = routes[k : k + 1, :] == number
        member = jnp.where(named, 1.0, member)
        weight = jnp.where(named, weights[k : k + 1, :], weight)
    before = lax.broadcasted_iota(jnp.int32, (tokens, tokens), 0)
    after = lax.broadcasted_iota(jnp.int32, (tokens, tokens), 1)
    earlier = jnp.where(before < after, 1.0, 0.0).astype(BF)
    slot = jnp.dot(member.astype(BF), earlier, preferred_element_type=F32)
    slot = jnp.where(member > 0.5, slot, -1.0)
    high = weight.astype(BF).astype(F32)
    rest = jnp.zeros((experts, lanes - 3 * tokens), F32)
    slot = jnp.concatenate([slot, slot, slot, rest - 1.0], axis=1)
    value = jnp.concatenate([member, high, weight - high, rest], axis=1)
    place = lax.broadcasted_iota(jnp.int32, (slots, lanes), 0).astype(F32)
    for e in range(experts):
        block = jnp.where(slot[e : e + 1] == place, value[e : e + 1], 0.0)
        at = e % side * slots
        meta[e // side, at : at + slots] = block.astype(BF)


def plan(planes):
    if planes == 4:
        order = [[0, 1, 3, 2], [1, 0, 2, 3], [2, 1, 3, 0], [3, 2, 1, 0]]
        route = [
            {0: [1], 1: [2], 2: [3]},
            {1: [2, 0], 2: [3]},
            {2: [3, 1], 1: [0]},
            {3: [2, 1], 1: [0]},
        ]
        early = [[1, 0, 0, 0], [1, 0, 1, 0], [1, 0, 0, 1], [1, 0, 0, 0]]
        steps = (
            "P0 S R1b R1a",
            "P1 F0 R2b R2a",
            "R3a F1 R3b P3",
            "C1 P2 F3 N1",
            "C3 F2 N3 M1",
            "C20 M3 N2 N0",
            "M2 M0",
        )
        return order, route, early, sum([line.split() for line in steps], [])
    order = [sorted(range(planes), key=lambda s: (abs(s - z), s)) for z in range(planes)]
    route = []
    for s in range(planes):
        hops = {z: [z + 1] for z in range(s, planes - 1)}
        hops.update({z: [z - 1] for z in range(1, s + 1)})
        hops[s] = [z for z in (s + 1, s - 1) if 0 <= z < planes]
        route.append(hops)
    early = [[1] * planes for _ in range(planes)]
    steps = ["P0", "S"]
    for t in range(planes + 2):
        for lag, kind in ((-1, "R"), (-1, "P"), (0, "F"), (0, "C"), (1, "N"), (2, "M")):
            if 0 <= t - lag < planes:
                steps.append(kind + str(t - lag) + "a" * (kind == "R"))
    return order, route, early, steps


def run_steps(script, pick, send_meta, relay, forward, compute, finish, combine):
    table = {"P": pick, "F": forward, "C": compute, "N": finish, "M": combine}
    for step in script:
        if step == "S":
            send_meta()
        elif step[0] == "R":
            relay(int(step[1]), int(step[2:] == "a"))
        else:
            table[step[0]](*[int(v) for v in step[1:]])


def choose(values, index):
    total = 0
    for i, value in enumerate(values):
        total = total + value * lax.div(1, 1 + (index - i) * (index - i))
    return total


def expert_kernel(
    planes,
    side,
    slots,
    lengths_hbm,
    routes_hbm,
    weights_hbm,
    drafts_hbm,
    residual_hbm,
    gain_hbm,
    q_hbm,
    cache_hbm,
    vup_hbm,
    gate_hbm,
    up_hbm,
    down_hbm,
    out,
    lengths,
    routes,
    weights,
    drafts,
    residual,
    gain,
    q_v,
    cache_v,
    vup,
    mixes,
    stream,
    meta,
    w_gate,
    w_up,
    w_down,
    z_rows,
    z_meta,
    stage,
    rows,
    mine,
    pair_out,
    pair_in,
    back_out,
    back_in,
    part_out,
    part_in,
    total,
    far_sem,
    s_sem,
    q_sem,
    c_sem,
    v_sem,
    w_sem,
    zr_s,
    zr_r,
    zm_s,
    zm_r,
    ip_s,
    ip_r,
    fw_s,
    fw_r,
    pp_s,
    pp_r,
    rt_s,
    rt_r,
    fn_s,
    fn_r,
):
    tokens, width = stream.shape
    pieces = zr_r.shape[1]
    piece = tokens // pieces
    qs = side * slots
    me = lax.axis_index("ep")
    core = lax.rem(me, 2)
    other = 1 - core
    chip = me // 2
    z = chip // side
    q = lax.rem(chip, side)

    def at(zz, qq, cc):
        return {"ep": (zz * side + qq) * 2 + cc}

    def remote(src, dst, send, recv, device):
        return pltpu.make_async_remote_copy(
            src_ref=src,
            dst_ref=dst,
            send_sem=send,
            recv_sem=recv,
            device_id=device,
            device_id_type=pl.DeviceIdType.MESH,
        )

    near, route, early, script = plan(planes)
    chunk = [z] + [choose([near[i][k] for i in range(planes)], z) for k in range(1, planes)]
    flips = [
        None,
        q + 1 - 2 * lax.rem(q, 2),
        lax.rem(q + 2, 4),
        3 - q,
    ]
    turns = [3, 1, 2][: side - 1]

    reqs, draft_heads, _ = q_v.shape
    small = [
        pltpu.make_async_copy(src, dst, s_sem.at[i])
        for i, (src, dst) in enumerate(
            [
                (routes_hbm, routes),
                (weights_hbm, weights),
                (drafts_hbm, drafts),
                (residual_hbm, residual),
                (gain_hbm, gain),
                (lengths_hbm, lengths),
            ]
        )
    ]
    for load in small[2:3] + small[5:]:
        load.start()
    fetched = []
    for r in range(reqs):
        pair = [
            pltpu.make_async_copy(q_hbm.at[r], q_v.at[r], q_sem.at[r]),
            pltpu.make_async_copy(cache_hbm.at[r], cache_v.at[r], c_sem.at[r]),
        ]
        for load in pair:
            load.start()
        fetched.append(pair)
    for load in small[:2] + small[3:5]:
        load.start()
    vup_load = pltpu.make_async_copy(vup_hbm, vup, v_sem.at[0])
    vup_load.start()
    loads = [
        pltpu.make_async_copy(gate_hbm.at[0], w_gate, w_sem.at[0]),
        pltpu.make_async_copy(up_hbm.at[0], w_up, w_sem.at[1]),
        pltpu.make_async_copy(down_hbm.at[0], w_down, w_sem.at[2]),
    ]
    for load in loads:
        load.start()

    def flag(test, k):
        return choose([int(test(i, near[i][k])) for i in range(planes)], z) == 1

    def signal(semaphore, device):
        pl.semaphore_signal(
            semaphore, inc=1, device_id=device, device_id_type=pl.DeviceIdType.MESH
        )

    barrier = pltpu.get_barrier_semaphore()
    for j in turns:
        signal(barrier, at(z, flips[j], core))
    signal(barrier, at(z, q, other))
    for k in range(1, planes):
        pl.when(flag(lambda i, d: d >= i - 1, k))(
            functools.partial(signal, barrier, at(chunk[k], q, core))
        )
    heard = [sum(s != i and s <= i + 1 for s in range(planes)) for i in range(planes)]

    for load in small[2:3] + small[5:]:
        load.wait()
    heads, latent, head = vup.shape
    scale = (head + q_v.shape[2] - latent) ** (-0.5)
    for r in range(reqs):
        if r == reqs - 1:
            pl.semaphore_wait(barrier, len(turns) + 1 + choose(heard, z))
            for k in range(1, planes):
                pl.when(flag(lambda i, d: d < i - 1, k))(
                    functools.partial(signal, far_sem.at[z], at(chunk[k], q, core))
                )
        for load in fetched[r]:
            load.wait()
        mixed = attend(q_v[r], cache_v[r], drafts[r], lengths[:, r : r + 1], heads, latent, scale)
        for g in range(latent // 128):
            mixes[g, r * draft_heads : (r + 1) * draft_heads] = mixed[
                :, g * 128 : (g + 1) * 128
            ]
    for load in small[:2] + small[3:5]:
        load.wait()
    tables(routes, weights, meta, slots)
    vup_load.wait()
    for h in range(heads):
        value = jnp.concatenate(
            [mixes[g, pl.ds(h, tokens, stride=heads), :] for g in range(latent // 128)], axis=1
        ).astype(BF)
        part = slice(h * head, (h + 1) * head)
        stream[:, part] = residual[:, part].astype(F32) + jnp.dot(
            value, vup[h], preferred_element_type=F32
        )
    value = stream[...]
    level = lax.rsqrt(jnp.mean(value * value, axis=-1, keepdims=True) + 1e-06)
    z_rows[z] = (value * level * gain[...]).astype(BF)
    sends = []
    returns = []

    def go(copy):
        copy.start()
        sends.append(copy)

    def hop(k, p, way, target, valid):
        s = chunk[k]
        place = z_rows.at[s, p * piece : (p + 1) * piece]
        copy = remote(place, place, zr_s.at[k, way, p], zr_r.at[s, p], at(target, q, core))
        pl.when(valid)(copy.start)

    def fans_of(k):
        return [route[near[i][k]].get(i, []) for i in range(planes)]

    def landed(k, p):
        s = chunk[k]
        place = z_rows.at[s, p * piece : (p + 1) * piece]
        return remote(place, place, zr_s.at[k, 0, p], zr_r.at[s, p], at(s, q, core))

    def onward(k):
        fans = fans_of(k)
        for p in range(pieces):
            if k:
                landed(k, p).wait_recv()
            for way in range(max(len(fan) for fan in fans)):
                valid = choose([int(way < len(fan)) for fan in fans], z)
                target = choose([(fan + [0] * (way + 1))[way] for fan in fans], z)
                hop(k, p, way, target, valid == 1)

    def relay(k, when):
        fans = fans_of(k)
        now = [int(bool(fan) and early[i][k] == when) for i, fan in enumerate(fans)]
        if any(now):
            pl.when(choose(now, z) == 1)(lambda: onward(k))

    def arrive(k):
        leaf = choose([int(not fan) for fan in fans_of(k)], z)

        @pl.when(leaf == 1)
        def _():
            for p in range(pieces):
                landed(k, p).wait_recv()

    onward(0)

    def send_meta():
        for k in range(1, planes):
            zd = chunk[k]
            pl.when(flag(lambda i, d: d > i + 1, k))(
                functools.partial(pl.semaphore_wait, far_sem.at[zd], 1)
            )
            go(remote(meta.at[zd], z_meta.at[z], zm_s.at[k], zm_r.at[z], at(zd, q, core)))

    def pick(k):
        s = chunk[k]
        if k:
            arrive(k)
            device = at(s, q, core)
            remote(z_meta.at[s], z_meta.at[s], zm_s.at[k], zm_r.at[s], device).wait_recv()
            table, values = z_meta[s], z_rows[s]
        else:
            table, values = meta[z], z_rows[z]
        picked = jnp.dot(table[:, :tokens], values, preferred_element_type=F32).astype(BF)
        stage[k] = picked.reshape(side, slots, width)
        for j in turns:
            go(
                remote(
                    stage.at[k, flips[j]],
                    rows.at[core, s, q],
                    ip_s.at[k, j],
                    ip_r.at[s, j],
                    at(z, flips[j], core),
                )
            )
        rows[core, s, q] = stage[k, q]
        cross(k, 0, q)

    def cross(k, j, qk):
        place = rows.at[core, chunk[k], qk]
        go(remote(place, place, fw_s.at[k, j], fw_r.at[chunk[k], j], at(z, q, other)))

    def forward(k):
        s = chunk[k]
        for j in turns[1:] + turns[:1]:
            landing = rows.at[core, s, flips[j]]
            remote(
                landing, landing, ip_s.at[k, j], ip_r.at[s, j], at(z, flips[j], core)
            ).wait_recv()
            cross(k, j, flips[j])

    def compute(*ks):
        for k in ks:
            s = chunk[k]
            for j in [0] + turns:
                landing = rows.at[other, s, flips[j] if j else q]
                remote(
                    landing, landing, fw_s.at[k, j], fw_r.at[s, j], at(z, q, other)
                ).wait_recv()
        while loads:
            loads.pop(0).wait()
        blocks = [rows[cc, chunk[k]].reshape(qs, width) for cc in (other, core) for k in ks]
        x = jnp.concatenate(blocks, axis=0)
        gate = dot_rows(x, w_gate[...])
        upper = dot_rows(x, w_up[...])
        active = (gate / (1.0 + jnp.exp(-gate)) * upper).astype(BF)
        half = width // 2
        for p in range(2):
            part = slice(p * half, (p + 1) * half)
            both = jnp.dot(active, w_down[:, part], preferred_element_type=F32)
            for i, k in enumerate(ks):
                s = chunk[k]
                pair_out[k, p] = both[i * qs : (i + 1) * qs].astype(BF)
                go(
                    remote(
                        pair_out.at[k, p],
                        pair_in.at[s, p],
                        pp_s.at[k, p],
                        pp_r.at[s, p],
                        at(z, q, other),
                    )
                )
                i += len(ks)
                mine[k, p] = both[i * qs : (i + 1) * qs]

    def finish(k):
        s = chunk[k]
        half = width // 2
        for p in range(2):
            landing = pair_in.at[s, p]
            remote(
                landing, landing, pp_s.at[k, p], pp_r.at[s, p], at(z, q, other)
            ).wait_recv()
            done = (mine[k, p] + pair_in[s, p].astype(F32)).astype(BF)
            back_out[k, :, :, p * half : (p + 1) * half] = done.reshape(side, slots, half)
        for j in turns:
            go(
                remote(
                    back_out.at[k, flips[j]],
                    back_in.at[s, q],
                    rt_s.at[k, j],
                    rt_r.at[s, j],
                    at(z, flips[j], core),
                )
            )
        back_in[s, q] = back_out[k, q]

    def combine(k):
        s = chunk[k]
        for j in turns:
            landing = back_in.at[s, flips[j]]
            remote(
                landing, landing, rt_s.at[k, j], rt_r.at[s, j], at(z, flips[j], core)
            ).wait_recv()
        table = z_meta[s] if k else meta[z]
        weigh = jnp.transpose(table.astype(F32))[tokens : 3 * tokens].astype(BF)
        values = back_in[s].reshape(qs, width)
        both = jnp.dot(weigh, values, preferred_element_type=F32)
        part = both[:tokens] + both[tokens:]
        if k:
            part_out[k] = part.astype(BF)
            copy = remote(
                part_out.at[k], part_in.at[z], fn_s.at[k], fn_r.at[z], at(s, q, core)
            )
            copy.start()
            returns.append(copy)
        else:
            total[...] = stream[...] + part

    run_steps(script, pick, send_meta, relay, forward, compute, finish, combine)

    for copy in sends:
        copy.wait_send()
    for k in range(planes):
        fans = fans_of(k)
        for p in range(pieces):
            for way in range(max(len(fan) for fan in fans)):
                valid = choose([int(way < len(fan)) for fan in fans], z)
                place = z_rows.at[chunk[k], p * piece : (p + 1) * piece]
                copy = remote(place, place, zr_s.at[k, way, p], zr_r.at[z, p], at(z, q, other))
                pl.when(valid == 1)(copy.wait_send)
    result = total[...]
    for k in range(1, planes):
        s = chunk[k]
        landing = part_in.at[s]
        remote(landing, landing, fn_s.at[k], fn_r.at[s], at(s, q, core)).wait_recv()
        result = result + part_in[s].astype(F32)
    out[...] = result.astype(BF)
    for copy in returns:
        copy.wait_send()


def local(
    queries,
    cache,
    drafts,
    lengths,
    value_up,
    residual,
    norm_gain,
    w_gate,
    w_up,
    w_down,
    routes,
    combine_weights,
):
    tokens, width = residual.shape
    top = routes.shape[1]
    hidden = w_gate.shape[2]
    reqs, draft, heads, key = queries.shape
    queries = queries.reshape(reqs, draft * heads, key)
    cache = jnp.transpose(cache, (0, 2, 1))
    w_gate = jnp.transpose(w_gate, (0, 2, 1))
    w_up = jnp.transpose(w_up, (0, 2, 1))
    experts = lax.axis_size("ep") // 2
    capacity = min(tokens, 2 * (((tokens * top + experts - 1) // experts + 3) // 2))
    slots = up_to(capacity, 16)
    side = 4 if experts % 4 == 0 else 1
    planes = experts // side
    qs = side * slots
    lanes = up_to(3 * tokens + 1, 128)
    vm = pl.BlockSpec(memory_space=pltpu.VMEM)
    hbm = pl.BlockSpec(memory_space=pl.ANY)
    dma = pltpu.SemaphoreType.DMA
    block = (planes, side, slots, width)
    return pl.pallas_call(
        functools.partial(expert_kernel, planes, side, slots),
        out_shape=pltpu.VMEM((tokens, width), BF),
        in_specs=[hbm] * 12,
        out_specs=vm,
        scratch_shapes=[
            pltpu.VMEM((1, reqs), lengths.dtype),
            pltpu.VMEM((routes.shape[1], tokens), routes.dtype),
            pltpu.VMEM((routes.shape[1], tokens), F32),
            pltpu.VMEM(drafts.shape, BF),
            pltpu.VMEM(residual.shape, BF),
            pltpu.VMEM((1, width), F32),
            pltpu.VMEM(queries.shape, BF),
            pltpu.VMEM(cache.shape, BF),
            pltpu.VMEM(value_up.shape, BF),
            pltpu.VMEM((value_up.shape[1] // 128, tokens * heads, 128), F32),
            pltpu.VMEM((tokens, width), F32),
            pltpu.VMEM((planes, qs, lanes), BF),
            pltpu.VMEM((hidden, width), BF),
            pltpu.VMEM((hidden, width), BF),
            pltpu.VMEM((hidden, width), BF),
            pltpu.VMEM((planes, tokens, width), BF),
            pltpu.VMEM((planes, qs, lanes), BF),
            pltpu.VMEM(block, BF),
            pltpu.VMEM((2,) + block, BF),
            pltpu.VMEM((planes, 2, qs, width // 2), F32),
            pltpu.VMEM((planes, 2, qs, width // 2), BF),
            pltpu.VMEM((planes, 2, qs, width // 2), BF),
            pltpu.VMEM(block, BF),
            pltpu.VMEM(block, BF),
            pltpu.VMEM((planes, tokens, width), BF),
            pltpu.VMEM((planes, tokens, width), BF),
            pltpu.VMEM((tokens, width), F32),
            pltpu.SemaphoreType.REGULAR((planes,)),
            dma((6,)),
            dma((reqs,)),
            dma((reqs,)),
            dma((1,)),
            dma((3,)),
        ]
        + [dma((planes, 3, 1)), dma((planes, 1))]
        + [dma((planes,))] * 2
        + [dma((planes, side))] * 4
        + [dma((planes, 2))] * 2
        + [dma((planes, side))] * 2
        + [dma((planes,))] * 2,
        compiler_params=pltpu.CompilerParams(
            collective_id=0, has_side_effects=True, vmem_limit_bytes=60 * 2**20
        ),
    )(
        lengths[None],
        routes.T,
        combine_weights.T,
        drafts,
        residual,
        norm_gain[None],
        queries,
        cache,
        value_up,
        w_gate,
        w_up,
        w_down,
    )


def solution(mesh):
    placed = (
        P(("groups", "ep"), None, None, None),
        P(("groups", "ep"), None, None),
        P(("groups", "ep"), None, None),
        P(("groups", "ep")),
        P(),
        P(("groups", "ep"), None),
        P(),
        P("ep", None, None),
        P("ep", None, None),
        P("ep", None, None),
        P(("groups", "ep"), None),
        P(("groups", "ep"), None),
    )
    return jax.shard_map(
        local, mesh=mesh, in_specs=placed, out_specs=P(("groups", "ep"), None), check_vma=False
    )
```
